32 devices in a mesh: blk: 4 (over y, x), rep: 8 (over z, core).
Axes of the slice: x: 2, y: 2, z: 4, core: 2. Of those that a mesh axis runs over, the one named last changes fastest.
Arguments:
- query_hidden: bfloat16 [8, 16, 32, 768], P('rep', 'blk'), may hold values from -18 to 18
- passage_hidden: bfloat16 [8, 16, 512, 768], P('rep', 'blk'), may hold values from -6 to 6
- lengths: int32 [8, 16], P('rep', 'blk'), may hold values from 64 to 512
- projection: bfloat16 [768, 128], replicated, may hold values from -0.21875 to 0.21875
Outputs:
- query_grad: float32 [8, 16, 32, 128], P('rep', 'blk')
- passage_grad: float32 [8, 16, 512, 128], P('rep', 'blk')
- grad_weight: float32 [768, 128], replicated
- loss: float32 [], replicated
The draws below stay inside these ranges and needn't reach their ends.
All inputs are finite; a program needn't handle non-finite values.
Results may differ from the reference program's by a relative error of at most 0.0097.
Values may be sent and summed in bfloat16 or wider, within the bound.
A program may use at most 128 MiB of HBM per device.

```python
import jax
import jax.numpy as jnp
from jax import lax

H = 768
DIM = 128
QLEN = 32
PLEN = 512
QN = 16
PN = 16
NQ_ALL = 128
N_REP = 8


def shared_passages(key):
    noise = jax.random.normal(jax.random.fold_in(key, 11), (N_REP, PN, PLEN, H), jnp.float32)
    values = jnp.clip(noise, -6.0, 6.0)
    return values


def draw_passage_hidden(key, part):
    return shared_passages(key).astype(jnp.bfloat16)


def draw_query_hidden(key, part):
    noise = jax.random.normal(jax.random.fold_in(key, 13), (N_REP, QN, QLEN, H), jnp.float32)
    values = 0.1 * jnp.clip(noise, -6.0, 6.0)
    return values.astype(jnp.bfloat16)


def touch_ends(values, stream_key, least, top_value):
    dims = values.shape
    spot = [jax.random.randint(jax.random.fold_in(stream_key, axis), (), 0, dims[axis]) for axis in range(len(dims))]
    values = values.at[tuple(spot)].set(least)
    longest = dims.index(max(dims))
    spot[longest] = (spot[longest] + 1) % dims[longest]
    return values.at[tuple(spot)].set(top_value)


def bell_draw(key, extent, width, reach, kind=jnp.bfloat16):
    values = jax.random.normal(key, extent, jnp.float32) * width
    return jnp.minimum(jnp.maximum(values, -reach), reach).astype(kind)


def setup_inputs(seed: int = 0) -> dict:
    key_list = jax.random.split(jax.random.key(seed), 5)
    query_hidden = draw_query_hidden(jax.random.fold_in(key_list[4], 71), 0)
    passage_hidden = draw_passage_hidden(jax.random.fold_in(key_list[4], 71), 0)
    lengths = touch_ends(jax.random.randint(key_list[2], (N_REP, PN), PLEN // 8, PLEN + 1), jax.random.fold_in(key_list[2], 1), PLEN // 8, PLEN).astype(jnp.int32)
    projection = bell_draw(key_list[3], (H, DIM), H ** -0.5, 0.21875)
    return dict(query_hidden=query_hidden, passage_hidden=passage_hidden, lengths=lengths, projection=projection)


temper = 0.5


def soft_scores(scores, lens):
    slots = scores.shape[-1]
    valid = lax.broadcasted_iota(jnp.int32, (lens.shape[0], slots), 1) < lens[:, None]
    scaled = jnp.where(valid[None], scores / temper, -jnp.inf)
    top = jnp.max(scaled, -1, keepdims=True)
    logz = top + jnp.log(jnp.sum(jnp.exp(scaled - top), -1, keepdims=True))
    pooled = temper * (logz[..., 0] - jnp.log(lens.astype(jnp.float32))[None])
    return pooled, scaled, logz


def group_step(inputs):
    qhid, phid, lens, projection = inputs
    hidden = projection.shape[0]
    qtok = jnp.dot(qhid.reshape(-1, hidden), projection, preferred_element_type=jnp.float32).astype(jnp.bfloat16)
    ptok = jnp.dot(phid.reshape(-1, hidden), projection, preferred_element_type=jnp.float32).astype(jnp.bfloat16)
    nquery = qhid.shape[0]
    qlen = qhid.shape[1]
    npass = phid.shape[0]
    plen = phid.shape[1]
    scores = jnp.dot(qtok, ptok.T, preferred_element_type=jnp.float32).reshape(nquery * qlen, npass, plen)
    pooled, scaled, logz = soft_scores(scores, lens)
    score = jnp.sum(pooled.reshape(nquery, qlen, npass), 1)
    top = jnp.max(score, 1, keepdims=True)
    lse = top + jnp.log(jnp.sum(jnp.exp(score - top), 1, keepdims=True))
    target = lax.broadcasted_iota(jnp.int32, score.shape, 1) == lax.broadcasted_iota(jnp.int32, score.shape, 0)
    loss_part = jnp.sum(lse[:, 0] - jnp.sum(jnp.where(target, score, 0.0), 1))
    dscore = (jnp.exp(score - lse) - target.astype(jnp.float32)) / NQ_ALL
    spread = jnp.repeat(dscore, qlen, axis=0)
    grad_a = (spread[:, :, None] * jnp.exp(scaled - logz)).astype(jnp.bfloat16).reshape(nquery * qlen, npass * plen)
    qgrad = jnp.dot(grad_a, ptok, preferred_element_type=jnp.float32)
    pgrad = jnp.dot(grad_a.T, qtok, preferred_element_type=jnp.float32)
    wgrad = jnp.dot(qhid.reshape(-1, hidden).T, qgrad.astype(jnp.bfloat16), preferred_element_type=jnp.float32)
    wgrad = wgrad + jnp.dot(phid.reshape(-1, hidden).T, pgrad.astype(jnp.bfloat16), preferred_element_type=jnp.float32)
    return qgrad.reshape(nquery, qlen, -1), pgrad.reshape(npass, plen, -1), wgrad, loss_part


def reference(query_hidden, passage_hidden, lengths, projection):
    copies = jnp.broadcast_to(projection, (query_hidden.shape[0],) + projection.shape)
    qgrad, pgrad, wgrad, losses = lax.map(group_step, (query_hidden, passage_hidden, lengths, copies))
    return qgrad, pgrad, jnp.sum(wgrad, 0), jnp.sum(losses) / NQ_ALL
```

```python
import functools

import jax
import jax.numpy as jnp
from jax import lax
from jax.experimental import pallas as pl
from jax.experimental.pallas import tpu as pltpu
from jax.sharding import PartitionSpec as P

MESH = pl.DeviceIdType.MESH
F32 = jnp.float32
BF16 = jnp.bfloat16
HIGH = lax.Precision.HIGHEST
NT = (((1,), (1,)), ((), ()))

temper = 0.5


def rows_iota(shape, dim):
    return lax.broadcasted_iota(jnp.int32, shape, dim)


def kernel(
    dims, lens, qhid, proj, phid, qg_out, pg_out, wg_out, loss_out,
    tok, ptok, ptok_t, phid_v, expo, grad_a, sums, pooled, sc, lo, qsend, qrecv, pg_v, pg_t,
    wsend, wrecv, zbuf, cbuf,
    in_sem, out_sem, tok_s, tok_r, sc_s, sc_r, lo_s, lo_r, qg_s, qg_r, ws_s, ws_r, z_s, z_r, c_s, c_r,
):
    nblk, nrep, ncore, nquery, qlen, npass, plen = dims
    ntok = nquery * qlen
    nqi = nblk * ntok
    nq_all = nblk * nquery
    nz = nrep // ncore
    na = nblk * ncore
    dim = proj.shape[1]
    total = nq_all * nrep
    blk = lax.axis_index("blk")
    rep = lax.axis_index("rep")
    core = lax.rem(rep, ncore)
    zed = rep // ncore
    me_a = blk * ncore + core

    def blk_peer(k):
        return (lax.rem(blk + k, nblk), rep)

    def rep_peer(k):
        return (blk, lax.rem(rep + k, nrep))

    def a_index(k):
        return lax.rem(me_a + k, na)

    def a_peer(k):
        other = a_index(k)
        return (other // ncore, zed * ncore + lax.rem(other, ncore))

    def z_peer(k):
        return (blk, lax.rem(zed + k, nz) * ncore + core)

    def share(src, dst, send, recv, peer, count):
        copies = []
        for k in range(1, count):
            copy = pltpu.make_async_remote_copy(
                src_ref=src(k), dst_ref=dst, send_sem=send.at[k - 1], recv_sem=recv.at[k - 1],
                device_id=peer(k), device_id_type=MESH,
            )
            copy.start()
            copies.append(copy)
        return copies

    loads = []
    for p in range(npass):
        load = pltpu.make_async_copy(phid.at[p], phid_v.at[p], in_sem.at[p])
        load.start()
        loads.append(load)

    barrier = pltpu.get_barrier_semaphore()
    greeted = 0
    for count, peer in ((na, a_peer), (nrep, rep_peer)):
        for k in range(1, count):
            pl.semaphore_signal(barrier, inc=1, device_id=peer(k), device_id_type=MESH)
            greeted += 1

    tok[blk] = jnp.dot(qhid[...], proj[...], preferred_element_type=F32).astype(BF16)
    pl.semaphore_wait(barrier, greeted)
    tok_copies = share(lambda k: tok.at[blk], tok.at[blk], tok_s, tok_r, blk_peer, nblk)

    pooled[...] = jnp.zeros_like(pooled)
    sums[...] = jnp.ones_like(sums)
    for p in range(npass):
        loads[p].wait()
        vec = jnp.dot(phid_v[p], proj[...], preferred_element_type=F32).astype(BF16)
        ptok[p] = vec
        ptok_t[p] = vec.T
    for copy in tok_copies:
        copy.wait_recv()
    every = tok[...].reshape(nqi, dim)

    def forward(p, carry):
        count = lens[0, p]
        a = lax.dot_general(ptok[p], every, NT, preferred_element_type=F32)
        valid = rows_iota(a.shape, 0) < count
        scaled = jnp.where(valid, a / temper, -jnp.inf)
        top = jnp.max(scaled, 0, keepdims=True)
        e = jnp.exp(scaled - top)
        expo[p] = e
        s = jnp.sum(e, 0, keepdims=True)
        sums[pl.ds(p, 1), :] = s
        size = jnp.log(jnp.full((1, nqi), count, jnp.int32).astype(F32))
        pooled[pl.ds(p, 1), :] = temper * (top + jnp.log(s) - size)
        return carry

    lax.fori_loop(0, npass, forward, 0)

    ppad = pooled.shape[0]
    qpad = sc.shape[2]
    owner = rows_iota((nqi, qpad), 1) * qlen
    token = rows_iota((nqi, qpad), 0)
    pick = ((token >= owner) & (token < owner + qlen)).astype(F32)
    own = jnp.dot(pooled[...], pick, precision=HIGH, preferred_element_type=F32)
    sc[blk] = own
    sc_copies = share(lambda k: sc.at[blk], sc.at[blk], sc_s, sc_r, blk_peer, nblk)
    owner_t = rows_iota((qpad, nqi), 0) * qlen
    token_t = rows_iota((qpad, nqi), 1)
    spread = ((token_t >= owner_t) & (token_t < owner_t + qlen)).astype(F32)
    inv = 1.0 / sums[...]
    for copy in sc_copies:
        copy.wait_recv()

    score = sc[...]
    row = rows_iota(score.shape, 1)
    lane = rows_iota(score.shape, 2)
    slot = rows_iota(score.shape, 0)
    live = row < npass
    hidden_score = jnp.where(live, score, -jnp.inf)
    top = jnp.max(jnp.max(hidden_score, 0), 0, keepdims=True)
    lse = top + jnp.log(jnp.sum(jnp.sum(jnp.exp(hidden_score - top[None]), 0), 0, keepdims=True))
    hit = live & (slot * npass + row == lane)
    aim = jnp.sum(jnp.sum(jnp.where(hit, score, 0.0), 0), 0, keepdims=True)
    gap = jnp.where(rows_iota(lse.shape, 1) < nq_all, lse - aim, 0.0)
    part = jnp.sum(gap, 1, keepdims=True)
    lo[rep] = jnp.broadcast_to(part, lo.shape[1:])
    lo_copies = share(lambda k: lo.at[rep], lo.at[rep], lo_s, lo_r, rep_peer, nrep)

    mine = rows_iota(own.shape, 0) + blk * npass == rows_iota(own.shape, 1)
    dscore = (jnp.exp(own - lse) - mine.astype(F32)) / total
    factor = jnp.dot(dscore, spread, precision=HIGH, preferred_element_type=F32) * inv
    sums[...] = factor

    def backward(p, acc):
        d = (expo[p] * sums[pl.ds(p, 1), :]).astype(BF16)
        grad_a[p] = d
        return acc + jnp.dot(ptok_t[p], d, preferred_element_type=F32)

    qg_t = lax.fori_loop(0, npass, backward, jnp.zeros((dim, nqi), F32))
    for b in range(nblk):
        qsend[b] = qg_t[:, b * ntok : (b + 1) * ntok]
    qrecv[blk] = qsend[blk]
    qg_copies = share(lambda k: qsend.at[lax.rem(blk + k, nblk)], qrecv.at[blk], qg_s, qg_r, blk_peer, nblk)

    def passages(p, acc):
        g = jnp.dot(grad_a[p], every, preferred_element_type=F32)
        pg_v[p] = g
        return acc + jnp.dot(g.astype(BF16).T, phid_v[p], preferred_element_type=F32)

    wg_t = lax.fori_loop(0, npass, passages, jnp.zeros((dim, qhid.shape[1]), F32))
    store = pltpu.make_async_copy(pg_v, pg_out, out_sem)
    store.start()
    for copy in qg_copies:
        copy.wait_recv()
    mine_t = jnp.sum(qrecv[...], 0)
    wg_t = wg_t + jnp.dot(mine_t.astype(BF16), qhid[...], preferred_element_type=F32)
    depth = dim // na
    for a in range(na):
        wsend[a] = wg_t[a * depth : (a + 1) * depth].astype(BF16)
    wrecv[me_a] = wsend[me_a]
    ws_copies = share(lambda k: wsend.at[a_index(k)], wrecv.at[me_a], ws_s, ws_r, a_peer, na)
    qg_out[...] = mine_t.T
    for copy in ws_copies:
        copy.wait_recv()
    zbuf[zed] = jnp.sum(wrecv[...].astype(F32), 0).astype(BF16)
    z_copies = share(lambda k: zbuf.at[zed], zbuf.at[zed], z_s, z_r, z_peer, nz)
    for copy in lo_copies:
        copy.wait_recv()
    loss_out[...] = jnp.sum(lo[...], 0) / total
    for copy in z_copies:
        copy.wait_recv()
    cbuf[me_a] = jnp.sum(zbuf[...].astype(F32), 0).astype(BF16)
    c_copies = share(lambda k: cbuf.at[me_a], cbuf.at[me_a], c_s, c_r, a_peer, na)
    for copy in tok_copies + sc_copies + lo_copies + qg_copies + ws_copies + z_copies:
        copy.wait_send()
    store.wait()
    for copy in c_copies:
        copy.wait_recv()
    for a in range(na):
        wg_out[a * depth : (a + 1) * depth, :] = cbuf[a].astype(F32)
    for copy in c_copies:
        copy.wait_send()


def shards(query_hidden, passage_hidden, lengths, projection):
    hidden, dim = projection.shape
    nquery, qlen = query_hidden.shape[1:3]
    npass, plen = passage_hidden.shape[1:3]
    nblk = lax.axis_size("blk")
    nrep = lax.axis_size("rep")
    ncore = 2 if nrep % 2 == 0 else 1
    nz = nrep // ncore
    na = nblk * ncore
    ntok = nquery * qlen
    nqi = nblk * ntok
    ppad = -(-npass // 8) * 8
    qpad = -(-nblk * nquery // 128) * 128
    dims = (nblk, nrep, ncore, nquery, qlen, npass, plen)
    vmem = pl.BlockSpec(memory_space=pltpu.VMEM)
    sem = lambda n: pltpu.SemaphoreType.DMA((max(n, 1),))
    pairs = []
    for n in (nblk, nblk, nrep, nblk, na, nz, na):
        pairs += [sem(n - 1), sem(n - 1)]
    qg, pg, wg_t, loss = pl.pallas_call(
        functools.partial(kernel, dims),
        out_shape=(
            jax.ShapeDtypeStruct((ntok, dim), F32),
            jax.ShapeDtypeStruct((npass, plen, dim), F32),
            jax.ShapeDtypeStruct((dim, hidden), F32),
            jax.ShapeDtypeStruct((8, 128), F32),
        ),
        in_specs=[
            pl.BlockSpec(memory_space=pltpu.SMEM), vmem, vmem, pl.BlockSpec(memory_space=pl.ANY),
        ],
        out_specs=(vmem, pl.BlockSpec(memory_space=pl.ANY), vmem, vmem),
        scratch_shapes=[
            pltpu.VMEM((nblk, ntok, dim), BF16),
            pltpu.VMEM((npass, plen, dim), BF16),
            pltpu.VMEM((npass, dim, plen), BF16),
            pltpu.VMEM((npass, plen, hidden), BF16),
            pltpu.VMEM((npass, plen, nqi), F32),
            pltpu.VMEM((npass, plen, nqi), BF16),
            pltpu.VMEM((ppad, nqi), F32),
            pltpu.VMEM((ppad, nqi), F32),
            pltpu.VMEM((nblk, ppad, qpad), F32),
            pltpu.VMEM((nrep, 8, 128), F32),
            pltpu.VMEM((nblk, dim, ntok), F32),
            pltpu.VMEM((nblk, dim, ntok), F32),
            pltpu.VMEM((npass, plen, dim), F32),
            pltpu.VMEM((dim, plen), BF16),
            pltpu.VMEM((na, dim // na, hidden), BF16),
            pltpu.VMEM((na, dim // na, hidden), BF16),
            pltpu.VMEM((nz, dim // na, hidden), BF16),
            pltpu.VMEM((na, dim // na, hidden), BF16),
            sem(npass),
            pltpu.SemaphoreType.DMA,
        ] + pairs,
        compiler_params=pltpu.CompilerParams(
            collective_id=0, has_side_effects=True, vmem_limit_bytes=56 << 20
        ),
    )(
        lengths,
        query_hidden.reshape(ntok, hidden),
        projection,
        passage_hidden.reshape(npass, plen, hidden),
    )
    return (
        qg.reshape(1, nquery, qlen, dim),
        pg.reshape(1, npass, plen, dim),
        wg_t.T,
        loss[0, 0],
    )


def solution(mesh):
    return jax.shard_map(
        shards,
        mesh=mesh,
        in_specs=(P("rep", "blk", None, None), P("rep", "blk", None, None), P("rep", "blk"), P()),
        out_specs=(P("rep", "blk", None, None), P("rep", "blk", None, None), P(), P()),
        check_vma=False,
    )
```

```python
import functools

import jax
import jax.numpy as jnp
from jax import lax
from jax.experimental import pallas as pl
from jax.experimental.pallas import tpu as pltpu
from jax.sharding import PartitionSpec as P

MESH = pl.DeviceIdType.MESH
F32 = jnp.float32
BF16 = jnp.bfloat16
HIGH = lax.Precision.HIGHEST
NT = (((1,), (1,)), ((), ()))

temper = 0.5


def rows_iota(shape, dim):
    return lax.broadcasted_iota(jnp.int32, shape, dim)


def kernel(
    dims, lens, qhid, proj, phid, qg_out, pg_v, cbuf, loss_out,
    tok, ptok, ptok_t, phid_v, expo, grad_a, sums, pooled, sc, lo, qsend, qrecv,
    wsend, wrecv, zbuf,
    in_sem, tok_s, tok_r, sc_s, sc_r, lo_s, lo_r, qg_s, qg_r, ws_s, ws_r, z_s, z_r, c_s, c_r,
):
    nblk, nrep, ncore, nquery, qlen, npass, plen = dims
    ntok = nquery * qlen
    nqi = nblk * ntok
    nq_all = nblk * nquery
    nz = nrep // ncore
    na = nblk * ncore
    dim = proj.shape[1]
    total = nq_all * nrep
    blk = lax.axis_index("blk")
    rep = lax.axis_index("rep")
    core = lax.rem(rep, ncore)
    zed = rep // ncore
    me_a = blk * ncore + core

    def blk_peer(k):
        return (lax.rem(blk + k, nblk), rep)

    def rep_peer(k):
        return (blk, lax.rem(rep + k, nrep))

    def a_index(k):
        return lax.rem(me_a + k, na)

    def a_peer(k):
        other = a_index(k)
        return (other // ncore, zed * ncore + lax.rem(other, ncore))

    def z_peer(k):
        return (blk, lax.rem(zed + k, nz) * ncore + core)

    def share(src, dst, send, recv, peer, count):
        copies = []
        for k in range(1, count):
            copy = pltpu.make_async_remote_copy(
                src_ref=src(k), dst_ref=dst, send_sem=send.at[k - 1], recv_sem=recv.at[k - 1],
                device_id=peer(k), device_id_type=MESH,
            )
            copy.start()
            copies.append(copy)
        return copies

    loads = []
    for p in range(npass):
        load = pltpu.make_async_copy(phid.at[p], phid_v.at[p], in_sem.at[p])
        load.start()
        loads.append(load)

    barrier = pltpu.get_barrier_semaphore()
    greeted = 0
    for count, peer in ((na, a_peer), (nrep, rep_peer)):
        for k in range(1, count):
            pl.semaphore_signal(barrier, inc=1, device_id=peer(k), device_id_type=MESH)
            greeted += 1

    tok[blk] = jnp.dot(qhid[...], proj[...], preferred_element_type=F32).astype(BF16)
    pl.semaphore_wait(barrier, greeted)
    tok_copies = share(lambda k: tok.at[blk], tok.at[blk], tok_s, tok_r, blk_peer, nblk)

    pooled[...] = jnp.zeros_like(pooled)
    sums[...] = jnp.ones_like(sums)
    for p in range(npass):
        loads[p].wait()
        vec = jnp.dot(phid_v[p], proj[...], preferred_element_type=F32).astype(BF16)
        ptok[p] = vec
        ptok_t[p] = vec.T
    for copy in tok_copies:
        copy.wait_recv()
    every = tok[...].reshape(nqi, dim)

    def forward(p, carry):
        count = lens[0, p]
        a = lax.dot_general(ptok[p], every, NT, preferred_element_type=F32)
        valid = rows_iota(a.shape, 0) < count
        scaled = jnp.where(valid, a / temper, -jnp.inf)
        top = jnp.max(scaled, 0, keepdims=True)
        e = jnp.exp(scaled - top)
        expo[p] = e
        s = jnp.sum(e, 0, keepdims=True)
        sums[pl.ds(p, 1), :] = s
        size = jnp.log(jnp.full((1, nqi), count, jnp.int32).astype(F32))
        pooled[pl.ds(p, 1), :] = temper * (top + jnp.log(s) - size)
        return carry

    lax.fori_loop(0, npass, forward, 0)

    ppad = pooled.shape[0]
    qpad = sc.shape[2]
    owner = rows_iota((nqi, qpad), 1) * qlen
    token = rows_iota((nqi, qpad), 0)
    pick = ((token >= owner) & (token < owner + qlen)).astype(F32)
    own = jnp.dot(pooled[...], pick, precision=HIGH, preferred_element_type=F32)
    sc[blk] = own
    sc_copies = share(lambda k: sc.at[blk], sc.at[blk], sc_s, sc_r, blk_peer, nblk)
    owner_t = rows_iota((qpad, nqi), 0) * qlen
    token_t = rows_iota((qpad, nqi), 1)
    spread = ((token_t >= owner_t) & (token_t < owner_t + qlen)).astype(F32)
    inv = 1.0 / sums[...]
    for copy in sc_copies:
        copy.wait_recv()

    score = sc[...]
    row = rows_iota(score.shape, 1)
    lane = rows_iota(score.shape, 2)
    slot = rows_iota(score.shape, 0)
    live = row < npass
    hidden_score = jnp.where(live, score, -jnp.inf)
    top = jnp.max(jnp.max(hidden_score, 0), 0, keepdims=True)
    lse = top + jnp.log(jnp.sum(jnp.sum(jnp.exp(hidden_score - top[None]), 0), 0, keepdims=True))
    hit = live & (slot * npass + row == lane)
    aim = jnp.sum(jnp.sum(jnp.where(hit, score, 0.0), 0), 0, keepdims=True)
    gap = jnp.where(rows_iota(lse.shape, 1) < nq_all, lse - aim, 0.0)
    part = jnp.sum(gap, 1, keepdims=True)
    lo[rep] = jnp.broadcast_to(part, lo.shape[1:])
    lo_copies = share(lambda k: lo.at[rep], lo.at[rep], lo_s, lo_r, rep_peer, nrep)

    mine = rows_iota(own.shape, 0) + blk * npass == rows_iota(own.shape, 1)
    dscore = (jnp.exp(own - lse) - mine.astype(F32)) / total
    factor = jnp.dot(dscore, spread, precision=HIGH, preferred_element_type=F32) * inv
    sums[...] = factor

    def backward(p, acc):
        d = (expo[p] * sums[pl.ds(p, 1), :]).astype(BF16)
        grad_a[p] = d
        return acc + jnp.dot(ptok_t[p], d, preferred_element_type=F32)

    qg_t = lax.fori_loop(0, npass, backward, jnp.zeros((dim, nqi), F32))
    for b in range(nblk):
        qsend[b] = qg_t[:, b * ntok : (b + 1) * ntok].astype(BF16)
    qrecv[blk] = qsend[blk]
    qg_copies = share(lambda k: qsend.at[lax.rem(blk + k, nblk)], qrecv.at[blk], qg_s, qg_r, blk_peer, nblk)

    def passages(p, acc):
        g = jnp.dot(grad_a[p], every, preferred_element_type=F32)
        pg_v[p] = g
        return acc + jnp.dot(g.astype(BF16).T, phid_v[p], preferred_element_type=F32)

    wg_t = lax.fori_loop(0, npass, passages, jnp.zeros((dim, qhid.shape[1]), F32))
    for copy in qg_copies:
        copy.wait_recv()
    mine_t = jnp.sum(qrecv[...].astype(F32), 0)
    wg_t = wg_t + jnp.dot(mine_t.astype(BF16), qhid[...], preferred_element_type=F32)
    depth = dim // na
    for a in range(na):
        wsend[a] = wg_t[a * depth : (a + 1) * depth].astype(BF16)
    wrecv[me_a] = wsend[me_a]
    ws_copies = share(lambda k: wsend.at[a_index(k)], wrecv.at[me_a], ws_s, ws_r, a_peer, na)
    qg_out[...] = mine_t.T
    for copy in ws_copies:
        copy.wait_recv()
    zbuf[zed] = jnp.sum(wrecv[...].astype(F32), 0).astype(BF16)
    z_copies = share(lambda k: zbuf.at[zed], zbuf.at[zed], z_s, z_r, z_peer, nz)
    for copy in lo_copies:
        copy.wait_recv()
    loss_out[...] = jnp.sum(lo[...], 0) / total
    for copy in z_copies:
        copy.wait_recv()
    cbuf[me_a] = jnp.sum(zbuf[...].astype(F32), 0).astype(BF16)
    c_copies = share(lambda k: cbuf.at[me_a], cbuf.at[me_a], c_s, c_r, a_peer, na)
    for copy in tok_copies + sc_copies + lo_copies + qg_copies + ws_copies + z_copies:
        copy.wait_send()
    for copy in c_copies:
        copy.wait_recv()
    for copy in c_copies:
        copy.wait_send()


def write_out(qg, pg, wg_t, loss, qg_out, pg_out, wg_out, loss_out, wg_v, sem):
    first = pltpu.make_async_copy(pg, pg_out, sem.at[0])
    first.start()
    second = pltpu.make_async_copy(qg, qg_out, sem.at[1])
    second.start()
    na, depth, hidden = wg_t.shape
    wg_v[...] = wg_t[...].astype(F32).reshape(na * depth, hidden).T
    third = pltpu.make_async_copy(wg_v, wg_out, sem.at[2])
    third.start()
    loss_out[0, 0] = loss[0, 0]
    first.wait()
    second.wait()
    third.wait()


def shards(query_hidden, passage_hidden, lengths, projection):
    hidden, dim = projection.shape
    nquery, qlen = query_hidden.shape[1:3]
    npass, plen = passage_hidden.shape[1:3]
    nblk = lax.axis_size("blk")
    nrep = lax.axis_size("rep")
    ncore = 2 if nrep % 2 == 0 else 1
    nz = nrep // ncore
    na = nblk * ncore
    ntok = nquery * qlen
    nqi = nblk * ntok
    ppad = -(-npass // 8) * 8
    qpad = -(-nblk * nquery // 128) * 128
    dims = (nblk, nrep, ncore, nquery, qlen, npass, plen)
    vmem = pl.BlockSpec(memory_space=pltpu.VMEM)
    sem = lambda n: pltpu.SemaphoreType.DMA((max(n, 1),))
    pairs = []
    for n in (nblk, nblk, nrep, nblk, na, nz, na):
        pairs += [sem(n - 1), sem(n - 1)]
    held = pl.pallas_call(
        functools.partial(kernel, dims),
        out_shape=(
            pltpu.VMEM((ntok, dim), F32),
            pltpu.VMEM((npass, plen, dim), F32),
            pltpu.VMEM((na, dim // na, hidden), BF16),
            pltpu.VMEM((8, 128), F32),
        ),
        in_specs=[
            pl.BlockSpec(memory_space=pltpu.SMEM), vmem, vmem, pl.BlockSpec(memory_space=pl.ANY),
        ],
        out_specs=(vmem, vmem, vmem, vmem),
        scratch_shapes=[
            pltpu.VMEM((nblk, ntok, dim), BF16),
            pltpu.VMEM((npass, plen, dim), BF16),
            pltpu.VMEM((npass, dim, plen), BF16),
            pltpu.VMEM((npass, plen, hidden), BF16),
            pltpu.VMEM((npass, plen, nqi), F32),
            pltpu.VMEM((npass, plen, nqi), BF16),
            pltpu.VMEM((ppad, nqi), F32),
            pltpu.VMEM((ppad, nqi), F32),
            pltpu.VMEM((nblk, ppad, qpad), F32),
            pltpu.VMEM((nrep, 8, 128), F32),
            pltpu.VMEM((nblk, dim, ntok), BF16),
            pltpu.VMEM((nblk, dim, ntok), BF16),
            pltpu.VMEM((na, dim // na, hidden), BF16),
            pltpu.VMEM((na, dim // na, hidden), BF16),
            pltpu.VMEM((nz, dim // na, hidden), BF16),
            sem(npass),
        ] + pairs,
        compiler_params=pltpu.CompilerParams(
            collective_id=0, has_side_effects=True, vmem_limit_bytes=56 << 20
        ),
    )(
        lengths,
        query_hidden.reshape(ntok, hidden),
        projection,
        passage_hidden.reshape(npass, plen, hidden),
    )
    hbm = pl.BlockSpec(memory_space=pl.ANY)
    qg, pg, wg, loss = pl.pallas_call(
        write_out,
        out_shape=(
            jax.ShapeDtypeStruct((ntok, dim), F32),
            jax.ShapeDtypeStruct((npass, plen, dim), F32),
            jax.ShapeDtypeStruct((hidden, dim), F32),
            jax.ShapeDtypeStruct((1, 1), F32),
        ),
        in_specs=[vmem] * 4,
        out_specs=(hbm, hbm, hbm, pl.BlockSpec(memory_space=pltpu.SMEM)),
        scratch_shapes=[pltpu.VMEM((hidden, dim), F32), sem(3)],
        compiler_params=pltpu.CompilerParams(vmem_limit_bytes=8 << 20),
    )(*[pltpu.with_memory_space_constraint(x, pltpu.VMEM) for x in held])
    return (
        qg.reshape(1, nquery, qlen, dim),
        pg.reshape(1, npass, plen, dim),
        wg,
        loss.reshape(()),
    )


def solution(mesh):
    return jax.shard_map(
        shards,
        mesh=mesh,
        in_specs=(P("rep", "blk", None, None), P("rep", "blk", None, None), P("rep", "blk"), P()),
        out_specs=(P("rep", "blk", None, None), P("rep", "blk", None, None), P(), P()),
        check_vma=False,
    )
```

```python
import functools

import jax
import jax.numpy as jnp
from jax import lax
from jax.experimental import pallas as pl
from jax.experimental.pallas import tpu as pltpu
from jax.sharding import PartitionSpec as P

MESH = pl.DeviceIdType.MESH
F32 = jnp.float32
BF16 = jnp.bfloat16
HIGH = lax.Precision.HIGHEST
NT = (((1,), (1,)), ((), ()))

temper = 0.5


def rows_iota(shape, dim):
    return lax.broadcasted_iota(jnp.int32, shape, dim)


def kernel(
    dims, lens_in, qhid_in, proj_in, phid_in, qg_out, pg_out, cbuf, loss_out,
    lens, qhid, proj, phid, tok, ptok, ptok_t, expo, grad_a, sums, tops, sc, lo, qsend, qrecv,
    wsend, wrecv, zbuf,
    in_sem, tok_s, tok_r, sc_s, sc_r, lo_s, lo_r, qg_s, qg_r, ws_s, ws_r, z_s, z_r, c_s, c_r,
):
    nblk, nrep, ncore, ncol, nquery, qlen, npass, plen = dims
    ntok = nquery * qlen
    nqi = nblk * ntok
    nq_all = nblk * nquery
    nz = nrep // ncore
    na = nblk * ncore
    nrow = nblk // ncol
    hidden, dim = proj.shape
    total = nq_all * nrep
    blk = lax.axis_index("blk")
    rep = lax.axis_index("rep")
    core = lax.rem(rep, ncore)
    zed = rep // ncore
    me_a = blk * ncore + core

    def blk_index(k):
        high = lax.rem(blk // ncol + k // ncol, nrow)
        low = lax.rem(lax.rem(blk, ncol) + k % ncol, ncol)
        return high * ncol + low

    def opposite(k):
        return (nrow - k // ncol) % nrow * ncol + (ncol - k % ncol) % ncol

    def blk_peer(k):
        return (blk_index(k), rep)

    def rep_peer(k):
        return (blk, lax.rem(rep + k, nrep))

    def a_index(k):
        return lax.rem(me_a + k, na)

    def a_peer(k):
        other = a_index(k)
        return (other // ncore, zed * ncore + lax.rem(other, ncore))

    def z_peer(k):
        return (blk, lax.rem(zed + k, nz) * ncore + core)

    def send(src, dst, send_sem, recv_sem, peer):
        copy = pltpu.make_async_remote_copy(
            src_ref=src, dst_ref=dst, send_sem=send_sem, recv_sem=recv_sem,
            device_id=peer, device_id_type=MESH,
        )
        copy.start()
        return copy

    def share(src, dst, send_sem, recv_sem, peer, count):
        return [
            send(src(k), dst, send_sem.at[k - 1], recv_sem.at[k - 1], peer(k)) for k in range(1, count)
        ]

    barrier = pltpu.get_barrier_semaphore()
    greeted = 0
    for count, peer in ((nrep, rep_peer), (na, a_peer)):
        for k in range(1, count):
            pl.semaphore_signal(barrier, inc=1, device_id=peer(k), device_id_type=MESH)
            greeted += 1

    loads = []
    pairs = [(qhid_in, qhid), (proj_in, proj), (lens_in, lens)]
    pairs += [(phid_in.at[p], phid.at[p]) for p in range(npass)]
    for n, (src, dst) in enumerate(pairs):
        load = pltpu.make_async_copy(src, dst, in_sem.at[n])
        load.start()
        loads.append(load)

    sums[...] = jnp.ones_like(sums)
    tops[...] = jnp.zeros_like(tops)
    loads[0].wait()
    loads[1].wait()
    tok[0] = jnp.dot(qhid[...], proj[...], preferred_element_type=F32).astype(BF16)
    pl.semaphore_wait(barrier, greeted)
    far = list(range(nblk - 1, 0, -1))
    tok_copies = {
        k: send(tok.at[0], tok.at[opposite(k)], tok_s.at[k - 1], tok_r.at[k - 1], blk_peer(k)) for k in far
    }

    loads[2].wait()
    ppad = sums.shape[1]
    qpad = sc.shape[2]
    size = jnp.ones((ppad, ntok), jnp.int32)
    for p in range(npass):
        size = jnp.where(rows_iota(size.shape, 0) == p, lens[0, p], size)
    log_size = jnp.log(size.astype(F32))
    for p in range(npass):
        loads[3 + p].wait()
        vec = jnp.dot(phid[p], proj[...], preferred_element_type=F32).astype(BF16)
        ptok[p] = vec
        ptok_t[p] = vec.T

    def forward(k):
        token = tok[k]

        def step(p, carry):
            a = lax.dot_general(ptok[p], token, NT, preferred_element_type=F32)
            valid = rows_iota(a.shape, 0) < lens[0, p]
            scaled = jnp.where(valid, a / temper, -jnp.inf)
            top = jnp.max(scaled, 0, keepdims=True)
            e = jnp.exp(scaled - top)
            expo[k, p] = e
            sums[k, pl.ds(p, 1), :] = jnp.sum(e, 0, keepdims=True)
            tops[k, pl.ds(p, 1), :] = top
            return carry

        lax.fori_loop(0, npass, step, 0)
        pooled = temper * (tops[k] + jnp.log(sums[k]) - log_size)
        query = rows_iota((ntok, qpad), 1) - blk_index(k) * nquery
        place = rows_iota((ntok, qpad), 0)
        pick = ((place >= query * qlen) & (place < (query + 1) * qlen)).astype(F32)
        return jnp.dot(pooled, pick, precision=HIGH, preferred_element_type=F32)

    own = forward(0)
    for k in range(1, nblk):
        tok_copies[opposite(k)].wait_recv()
        own = own + forward(k)
    sc[blk] = own
    sc_copies = [
        send(sc.at[blk], sc.at[blk], sc_s.at[k - 1], sc_r.at[k - 1], blk_peer(k)) for k in far
    ]
    for copy in sc_copies:
        copy.wait_recv()

    score = sc[...]
    row = rows_iota(score.shape, 1)
    lane = rows_iota(score.shape, 2)
    slot = rows_iota(score.shape, 0)
    live = row < npass
    hidden_score = jnp.where(live, score, -jnp.inf)
    top = jnp.max(jnp.max(hidden_score, 0), 0, keepdims=True)
    lse = top + jnp.log(jnp.sum(jnp.sum(jnp.exp(hidden_score - top[None]), 0), 0, keepdims=True))
    mine = rows_iota(own.shape, 0) + blk * npass == rows_iota(own.shape, 1)
    dscore = (jnp.exp(own - lse) - mine.astype(F32)) / total

    def backward(k):
        query = rows_iota((qpad, ntok), 0) - blk_index(k) * nquery
        place = rows_iota((qpad, ntok), 1)
        spread = ((place >= query * qlen) & (place < (query + 1) * qlen)).astype(F32)
        sums[k] = jnp.dot(dscore, spread, precision=HIGH, preferred_element_type=F32) / sums[k]

        def step(p, acc):
            d = (expo[k, p] * sums[k, pl.ds(p, 1), :]).astype(BF16)
            grad_a[p, :, k * ntok : (k + 1) * ntok] = d
            return acc + jnp.dot(ptok_t[p], d, preferred_element_type=F32)

        return lax.fori_loop(0, npass, step, jnp.zeros((dim, ntok), F32))

    qg_copies = []
    for k in far:
        qsend[k] = backward(k).astype(BF16)
        qg_copies.append(
            send(qsend.at[k], qrecv.at[opposite(k)], qg_s.at[k - 1], qg_r.at[k - 1], blk_peer(k))
        )
    mine_t = backward(0)

    hit = live & (slot * npass + row == lane)
    aim = jnp.sum(jnp.sum(jnp.where(hit, score, 0.0), 0), 0, keepdims=True)
    gap = jnp.where(rows_iota(lse.shape, 1) < nq_all, lse - aim, 0.0)
    part = jnp.sum(gap, 1, keepdims=True)
    lo[rep] = jnp.broadcast_to(part, lo.shape[1:])
    lo_copies = share(lambda k: lo.at[rep], lo.at[rep], lo_s, lo_r, rep_peer, nrep)

    every = tok[...].reshape(nqi, dim)

    def passages(p, acc):
        g = jnp.dot(grad_a[p], every, preferred_element_type=F32)
        pg_out[p] = g
        return acc + jnp.dot(g.astype(BF16).T, phid[p], preferred_element_type=F32)

    wg_t = lax.fori_loop(0, npass, passages, jnp.zeros((dim, hidden), F32))
    for copy in qg_copies:
        copy.wait_recv()
    for k in range(1, nblk):
        mine_t = mine_t + qrecv[k].astype(F32)
    wg_t = wg_t + jnp.dot(mine_t.astype(BF16), qhid[...], preferred_element_type=F32)
    depth = dim // na
    halves = range(wsend.shape[0])
    width = wsend.shape[3]
    ws_copies = []
    for h in halves:
        for a in range(na):
            wsend[h, a] = wg_t[a * depth : (a + 1) * depth, h * width : (h + 1) * width].astype(BF16)
        wrecv[h, me_a] = wsend[h, me_a]
        ws_copies.append(
            share(
                lambda k: wsend.at[h, a_index(k)], wrecv.at[h, me_a], ws_s.at[h], ws_r.at[h], a_peer, na
            )
        )
    qg_out[...] = mine_t.T
    z_copies = []
    for h in halves:
        for copy in ws_copies[h]:
            copy.wait_recv()
        zbuf[h, zed] = jnp.sum(wrecv[h].astype(F32), 0).astype(BF16)
        z_copies.append(
            share(lambda k: zbuf.at[h, zed], zbuf.at[h, zed], z_s.at[h], z_r.at[h], z_peer, nz)
        )
    for copy in lo_copies:
        copy.wait_recv()
    loss_out[...] = jnp.sum(lo[...], 0) / total
    c_copies = []
    for h in halves:
        for copy in z_copies[h]:
            copy.wait_recv()
        cbuf[h, me_a] = jnp.sum(zbuf[h].astype(F32), 0).astype(BF16)
        c_copies.append(
            share(lambda k: cbuf.at[h, me_a], cbuf.at[h, me_a], c_s.at[h], c_r.at[h], a_peer, na)
        )
    for copy in list(tok_copies.values()) + sc_copies + lo_copies + qg_copies:
        copy.wait_send()
    for h in halves:
        for copy in ws_copies[h] + z_copies[h]:
            copy.wait_send()
    for h in halves:
        for copy in c_copies[h]:
            copy.wait()


def write_out(qg, pg, wg_t, loss, qg_out, pg_out, wg_out, loss_out, wg_v, sem):
    copies = [pltpu.make_async_copy(pg.at[p], pg_out.at[p], sem.at[p]) for p in range(pg.shape[0])]
    copies.append(pltpu.make_async_copy(qg, qg_out, sem.at[pg.shape[0]]))
    for copy in copies:
        copy.start()
    nhalf, na, depth, width = wg_t.shape
    for h in range(nhalf):
        rows = slice(h * width, (h + 1) * width)
        wg_v[rows, :] = wg_t[h].astype(F32).reshape(na * depth, width).T
        copy = pltpu.make_async_copy(wg_v.at[rows], wg_out.at[rows], sem.at[pg.shape[0] + 1 + h])
        copy.start()
        copies.append(copy)
    loss_out[0, 0] = loss[0, 0]
    for copy in copies:
        copy.wait()


def shards(query_hidden, passage_hidden, lengths, projection):
    hidden, dim = projection.shape
    nquery, qlen = query_hidden.shape[1:3]
    npass, plen = passage_hidden.shape[1:3]
    nblk = lax.axis_size("blk")
    nrep = lax.axis_size("rep")
    ncore = 2 if nrep % 2 == 0 else 1
    ncol = 2 if nblk % 2 == 0 else 1
    nhalf = 2 if hidden % 256 == 0 else 1
    nz = nrep // ncore
    na = nblk * ncore
    ntok = nquery * qlen
    nqi = nblk * ntok
    ppad = -(-npass // 8) * 8
    qpad = -(-nblk * nquery // 128) * 128
    dims = (nblk, nrep, ncore, ncol, nquery, qlen, npass, plen)
    vmem = pl.BlockSpec(memory_space=pltpu.VMEM)
    hbm = pl.BlockSpec(memory_space=pl.ANY)
    piece = (dim // na, hidden // nhalf)
    sem = lambda *n: pltpu.SemaphoreType.DMA(n)
    pairs = []
    for n in (nblk, nblk, nrep, nblk):
        pairs += [sem(max(n - 1, 1)), sem(max(n - 1, 1))]
    for n in (na, nz, na):
        pairs += [sem(nhalf, max(n - 1, 1)), sem(nhalf, max(n - 1, 1))]
    held = pl.pallas_call(
        functools.partial(kernel, dims),
        out_shape=(
            pltpu.VMEM((ntok, dim), F32),
            pltpu.VMEM((npass, plen, dim), F32),
            pltpu.VMEM((nhalf, na) + piece, BF16),
            pltpu.VMEM((8, 128), F32),
        ),
        in_specs=[hbm] * 4,
        out_specs=(vmem, vmem, vmem, vmem),
        scratch_shapes=[
            pltpu.SMEM((1, npass), jnp.int32),
            pltpu.VMEM((ntok, hidden), BF16),
            pltpu.VMEM((hidden, dim), BF16),
            pltpu.VMEM((npass, plen, hidden), BF16),
            pltpu.VMEM((nblk, ntok, dim), BF16),
            pltpu.VMEM((npass, plen, dim), BF16),
            pltpu.VMEM((npass, dim, plen), BF16),
            pltpu.VMEM((nblk, npass, plen, ntok), F32),
            pltpu.VMEM((npass, plen, nqi), BF16),
            pltpu.VMEM((nblk, ppad, ntok), F32),
            pltpu.VMEM((nblk, ppad, ntok), F32),
            pltpu.VMEM((nblk, ppad, qpad), F32),
            pltpu.VMEM((nrep, 8, 128), F32),
            pltpu.VMEM((nblk, dim, ntok), BF16),
            pltpu.VMEM((nblk, dim, ntok), BF16),
            pltpu.VMEM((nhalf, na) + piece, BF16),
            pltpu.VMEM((nhalf, na) + piece, BF16),
            pltpu.VMEM((nhalf, nz) + piece, BF16),
            sem(npass + 3),
        ] + pairs,
        compiler_params=pltpu.CompilerParams(
            collective_id=0, has_side_effects=True, vmem_limit_bytes=56 << 20
        ),
    )(
        lengths,
        query_hidden.reshape(ntok, hidden),
        projection,
        passage_hidden.reshape(npass, plen, hidden),
    )
    qg, pg, wg, loss = pl.pallas_call(
        write_out,
        out_shape=(
            jax.ShapeDtypeStruct((ntok, dim), F32),
            jax.ShapeDtypeStruct((npass, plen, dim), F32),
            jax.ShapeDtypeStruct((hidden, dim), F32),
            jax.ShapeDtypeStruct((1, 1), F32),
        ),
        in_specs=[vmem] * 4,
        out_specs=(hbm, hbm, hbm, pl.BlockSpec(memory_space=pltpu.SMEM)),
        scratch_shapes=[pltpu.VMEM((hidden, dim), F32), sem(npass + 1 + nhalf)],
        compiler_params=pltpu.CompilerParams(vmem_limit_bytes=8 << 20),
    )(*[pltpu.with_memory_space_constraint(x, pltpu.VMEM) for x in held])
    return (
        qg.reshape(1, nquery, qlen, dim),
        pg.reshape(1, npass, plen, dim),
        wg,
        loss.reshape(()),
    )


def solution(mesh):
    return jax.shard_map(
        shards,
        mesh=mesh,
        in_specs=(P("rep", "blk", None, None), P("rep", "blk", None, None), P("rep", "blk"), P()),
        out_specs=(P("rep", "blk", None, None), P("rep", "blk", None, None), P(), P()),
        check_vma=False,
    )
```

```python
import functools

import jax
import jax.numpy as jnp
from jax import lax
from jax.experimental import pallas as pl
from jax.experimental.pallas import tpu as pltpu
from jax.sharding import PartitionSpec as P

MESH = pl.DeviceIdType.MESH
F32 = jnp.float32
BF16 = jnp.bfloat16
NT = (((1,), (1,)), ((), ()))

temper = 0.5


def rows_iota(shape, dim):
    return lax.broadcasted_iota(jnp.int32, shape, dim)


def exact_dot(x, ones):
    high = x.astype(BF16)
    rest = x - high.astype(F32)
    mid = rest.astype(BF16)
    low = (rest - mid.astype(F32)).astype(BF16)
    dot = lambda y: jnp.dot(y, ones, preferred_element_type=F32)
    return dot(high) + (dot(mid) + dot(low))


def kernel(
    dims, lens_in, qhid_in, proj_in, phid, qg_out, pg_v, cbuf, loss_out,
    lens, qhid, proj, pick, spread, tok, ptok, ptok_t, phid_v, expo, grad_a, sums, pooled, sc, lo, qsend, qrecv,
    wsend, wrecv, zbuf,
    in_sem, tok_s, tok_r, sc_s, sc_r, lo_s, lo_r, qg_s, qg_r, ws_s, ws_r, z_s, z_r, c_s, c_r,
):
    nblk, nrep, ncore, nquery, qlen, npass, plen = dims
    ntok = nquery * qlen
    nqi = nblk * ntok
    nq_all = nblk * nquery
    nz = nrep // ncore
    na = nblk * ncore
    dim = proj.shape[1]
    total = nq_all * nrep
    blk = lax.axis_index("blk")
    rep = lax.axis_index("rep")
    core = lax.rem(rep, ncore)
    zed = rep // ncore
    me_a = blk * ncore + core

    def blk_peer(k):
        return (lax.rem(blk + k, nblk), rep)

    def rep_peer(k):
        return (blk, lax.rem(rep + k, nrep))

    def a_index(k):
        return lax.rem(me_a + k, na)

    def a_peer(k):
        other = a_index(k)
        return (other // ncore, zed * ncore + lax.rem(other, ncore))

    def z_peer(k):
        return (blk, lax.rem(zed + k, nz) * ncore + core)

    def share(src, dst, send, recv, peer, count):
        copies = []
        for k in range(1, count):
            copy = pltpu.make_async_remote_copy(
                src_ref=src(k), dst_ref=dst, send_sem=send.at[k - 1], recv_sem=recv.at[k - 1],
                device_id=peer(k), device_id_type=MESH,
            )
            copy.start()
            copies.append(copy)
        return copies

    barrier = pltpu.get_barrier_semaphore()
    greeted = 0
    for count, peer in ((na, a_peer), (nrep, rep_peer)):
        for k in range(1, count):
            pl.semaphore_signal(barrier, inc=1, device_id=peer(k), device_id_type=MESH)
            greeted += 1

    loads = []
    pairs = [(qhid_in, qhid), (proj_in, proj), (lens_in, lens)]
    pairs += [(phid.at[p], phid_v.at[p]) for p in range(npass)]
    for n, (src, dst) in enumerate(pairs):
        load = pltpu.make_async_copy(src, dst, in_sem.at[n])
        load.start()
        loads.append(load)
    qpad = sc.shape[2]
    owner = rows_iota((nqi, qpad), 1) * qlen
    token = rows_iota((nqi, qpad), 0)
    pick[...] = jnp.where((token >= owner) & (token < owner + qlen), 1.0, 0.0).astype(BF16)
    owner_t = rows_iota((qpad, nqi), 0) * qlen
    token_t = rows_iota((qpad, nqi), 1)
    spread[...] = jnp.where((token_t >= owner_t) & (token_t < owner_t + qlen), 1.0, 0.0).astype(BF16)
    pooled[...] = jnp.zeros_like(pooled)
    sums[...] = jnp.ones_like(sums)
    loads[0].wait()
    loads[1].wait()
    tok[blk] = jnp.dot(qhid[...], proj[...], preferred_element_type=F32).astype(BF16)
    pl.semaphore_wait(barrier, greeted)
    tok_copies = share(lambda k: tok.at[blk], tok.at[blk], tok_s, tok_r, blk_peer, nblk)

    loads[2].wait()
    for p in range(npass):
        loads[3 + p].wait()
        vec = jnp.dot(phid_v[p], proj[...], preferred_element_type=F32).astype(BF16)
        ptok[p] = vec
        ptok_t[p] = vec.T
    for copy in tok_copies:
        copy.wait_recv()
    every = tok[...].reshape(nqi, dim)

    def forward(p, carry):
        count = lens[0, p]
        a = lax.dot_general(ptok[p], every, NT, preferred_element_type=F32)
        valid = rows_iota(a.shape, 0) < count
        scaled = jnp.where(valid, a / temper, -jnp.inf)
        top = jnp.max(scaled, 0, keepdims=True)
        e = jnp.exp(scaled - top)
        expo[p] = e
        s = jnp.sum(e, 0, keepdims=True)
        sums[pl.ds(p, 1), :] = s
        size = jnp.log(jnp.full((1, nqi), count, jnp.int32).astype(F32))
        pooled[pl.ds(p, 1), :] = temper * (top + jnp.log(s) - size)
        return carry

    lax.fori_loop(0, npass, forward, 0)

    own = exact_dot(pooled[...], pick[...])
    sc[blk] = own
    sc_copies = share(lambda k: sc.at[blk], sc.at[blk], sc_s, sc_r, blk_peer, nblk)
    inv = 1.0 / sums[...]
    for copy in sc_copies:
        copy.wait_recv()

    score = sc[...]
    row = rows_iota(score.shape, 1)
    lane = rows_iota(score.shape, 2)
    slot = rows_iota(score.shape, 0)
    live = row < npass
    hidden_score = jnp.where(live, score, -jnp.inf)
    top = jnp.max(jnp.max(hidden_score, 0), 0, keepdims=True)
    lse = top + jnp.log(jnp.sum(jnp.sum(jnp.exp(hidden_score - top[None]), 0), 0, keepdims=True))
    mine = rows_iota(own.shape, 0) + blk * npass == rows_iota(own.shape, 1)
    dscore = (jnp.exp(own - lse) - mine.astype(F32)) / total
    factor = exact_dot(dscore, spread[...]) * inv
    sums[...] = factor

    def backward(p, acc):
        d = (expo[p] * sums[pl.ds(p, 1), :]).astype(BF16)
        grad_a[p] = d
        return acc + jnp.dot(ptok_t[p], d, preferred_element_type=F32)

    qg_t = lax.fori_loop(0, npass, backward, jnp.zeros((dim, nqi), F32))
    for b in range(nblk):
        qsend[b] = qg_t[:, b * ntok : (b + 1) * ntok].astype(BF16)
    qrecv[blk] = qsend[blk]
    qg_copies = share(lambda k: qsend.at[lax.rem(blk + k, nblk)], qrecv.at[blk], qg_s, qg_r, blk_peer, nblk)

    hit = live & (slot * npass + row == lane)
    aim = jnp.sum(jnp.sum(jnp.where(hit, score, 0.0), 0), 0, keepdims=True)
    gap = jnp.where(rows_iota(lse.shape, 1) < nq_all, lse - aim, 0.0)
    part = jnp.sum(gap, 1, keepdims=True)
    lo[rep] = jnp.broadcast_to(part, lo.shape[1:])
    lo_copies = share(lambda k: lo.at[rep], lo.at[rep], lo_s, lo_r, rep_peer, nrep)


    def passages(p, acc):
        g = jnp.dot(grad_a[p], every, preferred_element_type=F32)
        pg_v[p] = g
        return acc + jnp.dot(g.astype(BF16).T, phid_v[p], preferred_element_type=F32)

    wg_t = lax.fori_loop(0, npass, passages, jnp.zeros((dim, qhid.shape[1]), F32))
    for copy in qg_copies:
        copy.wait_recv()
    mine_t = jnp.sum(qrecv[...].astype(F32), 0)
    wg_t = wg_t + jnp.dot(mine_t.astype(BF16), qhid[...], preferred_element_type=F32)
    depth = dim // na
    for a in range(na):
        wsend[a] = wg_t[a * depth : (a + 1) * depth].astype(BF16)
    wrecv[me_a] = wsend[me_a]
    ws_copies = share(lambda k: wsend.at[a_index(k)], wrecv.at[me_a], ws_s, ws_r, a_peer, na)
    qg_out[...] = mine_t.T
    for copy in ws_copies:
        copy.wait_recv()
    zbuf[zed] = jnp.sum(wrecv[...].astype(F32), 0).astype(BF16)
    z_copies = share(lambda k: zbuf.at[zed], zbuf.at[zed], z_s, z_r, z_peer, nz)
    for copy in lo_copies:
        copy.wait_recv()
    loss_out[...] = jnp.sum(lo[...], 0) / total
    for copy in z_copies:
        copy.wait_recv()
    cbuf[me_a] = jnp.sum(zbuf[...].astype(F32), 0).astype(BF16)
    c_copies = share(lambda k: cbuf.at[me_a], cbuf.at[me_a], c_s, c_r, a_peer, na)
    for copy in tok_copies + sc_copies + lo_copies + qg_copies + ws_copies + z_copies:
        copy.wait_send()
    for copy in c_copies:
        copy.wait_recv()
    for copy in c_copies:
        copy.wait_send()


def write_out(qg, pg, wg_t, loss, qg_out, pg_out, wg_out, loss_out, wg_v, sem):
    first = pltpu.make_async_copy(pg, pg_out, sem.at[0])
    first.start()
    second = pltpu.make_async_copy(qg, qg_out, sem.at[1])
    second.start()
    na, depth, hidden = wg_t.shape
    wg_v[...] = wg_t[...].astype(F32).reshape(na * depth, hidden).T
    third = pltpu.make_async_copy(wg_v, wg_out, sem.at[2])
    third.start()
    loss_out[0, 0] = loss[0, 0]
    first.wait()
    second.wait()
    third.wait()


def shards(query_hidden, passage_hidden, lengths, projection):
    hidden, dim = projection.shape
    nquery, qlen = query_hidden.shape[1:3]
    npass, plen = passage_hidden.shape[1:3]
    nblk = lax.axis_size("blk")
    nrep = lax.axis_size("rep")
    ncore = 2 if nrep % 2 == 0 else 1
    nz = nrep // ncore
    na = nblk * ncore
    ntok = nquery * qlen
    nqi = nblk * ntok
    ppad = -(-npass // 8) * 8
    qpad = -(-nblk * nquery // 128) * 128
    dims = (nblk, nrep, ncore, nquery, qlen, npass, plen)
    vmem = pl.BlockSpec(memory_space=pltpu.VMEM)
    sem = lambda n: pltpu.SemaphoreType.DMA((max(n, 1),))
    pairs = []
    for n in (nblk, nblk, nrep, nblk, na, nz, na):
        pairs += [sem(n - 1), sem(n - 1)]
    held = pl.pallas_call(
        functools.partial(kernel, dims),
        out_shape=(
            pltpu.VMEM((ntok, dim), F32),
            pltpu.VMEM((npass, plen, dim), F32),
            pltpu.VMEM((na, dim // na, hidden), BF16),
            pltpu.VMEM((8, 128), F32),
        ),
        in_specs=[
            *[pl.BlockSpec(memory_space=pl.ANY)] * 4,
        ],
        out_specs=(vmem, vmem, vmem, vmem),
        scratch_shapes=[
            pltpu.SMEM((1, npass), jnp.int32),
            pltpu.VMEM((ntok, hidden), BF16),
            pltpu.VMEM((hidden, dim), BF16),
            pltpu.VMEM((nqi, qpad), BF16),
            pltpu.VMEM((qpad, nqi), BF16),
            pltpu.VMEM((nblk, ntok, dim), BF16),
            pltpu.VMEM((npass, plen, dim), BF16),
            pltpu.VMEM((npass, dim, plen), BF16),
            pltpu.VMEM((npass, plen, hidden), BF16),
            pltpu.VMEM((npass, plen, nqi), F32),
            pltpu.VMEM((npass, plen, nqi), BF16),
            pltpu.VMEM((ppad, nqi), F32),
            pltpu.VMEM((ppad, nqi), F32),
            pltpu.VMEM((nblk, ppad, qpad), F32),
            pltpu.VMEM((nrep, 8, 128), F32),
            pltpu.VMEM((nblk, dim, ntok), BF16),
            pltpu.VMEM((nblk, dim, ntok), BF16),
            pltpu.VMEM((na, dim // na, hidden), BF16),
            pltpu.VMEM((na, dim // na, hidden), BF16),
            pltpu.VMEM((nz, dim // na, hidden), BF16),
            sem(npass + 3),
        ] + pairs,
        compiler_params=pltpu.CompilerParams(
            collective_id=0, has_side_effects=True, vmem_limit_bytes=56 << 20
        ),
    )(
        lengths,
        query_hidden.reshape(ntok, hidden),
        projection,
        passage_hidden.reshape(npass, plen, hidden),
    )
    hbm = pl.BlockSpec(memory_space=pl.ANY)
    qg, pg, wg, loss = pl.pallas_call(
        write_out,
        out_shape=(
            jax.ShapeDtypeStruct((ntok, dim), F32),
            jax.ShapeDtypeStruct((npass, plen, dim), F32),
            jax.ShapeDtypeStruct((hidden, dim), F32),
            jax.ShapeDtypeStruct((1, 1), F32),
        ),
        in_specs=[vmem] * 4,
        out_specs=(hbm, hbm, hbm, pl.BlockSpec(memory_space=pltpu.SMEM)),
        scratch_shapes=[pltpu.VMEM((hidden, dim), F32), sem(3)],
        compiler_params=pltpu.CompilerParams(vmem_limit_bytes=8 << 20),
    )(*[pltpu.with_memory_space_constraint(x, pltpu.VMEM) for x in held])
    return (
        qg.reshape(1, nquery, qlen, dim),
        pg.reshape(1, npass, plen, dim),
        wg,
        loss.reshape(()),
    )


def solution(mesh):
    return jax.shard_map(
        shards,
        mesh=mesh,
        in_specs=(P("rep", "blk", None, None), P("rep", "blk", None, None), P("rep", "blk"), P()),
        out_specs=(P("rep", "blk", None, None), P("rep", "blk", None, None), P(), P()),
        check_vma=False,
    )
```
